32 devices in a mesh: dp: 4 (over x, core), pipe: 8 (over z, y).
Axes of the slice: x: 2, y: 2, z: 4, core: 2. Of those that a mesh axis runs over, the one named last changes fastest.
Arguments:
- pre: bfloat16 [512, 49152], P('dp', 'pipe'), may hold values from -6 to 6
- grad_out: bfloat16 [512, 6144], P('dp', 'pipe'), may hold values from -6 to 6
- weight_slots: bfloat16 [8, 292, 128, 128], P('pipe', 'dp'), may hold values from -0.21875 to 0.21875
- block_rows: int32 [8, 292], P('pipe', 'dp'), may hold values from 0 to 47, as said below
- block_cols: int32 [8, 292], P('pipe', 'dp'), may hold values from 0 to 47, as said below
- block_count: int32 [8, 4], P('pipe', 'dp'), may hold values from 0 to 73, as said below
Outputs:
- pre_grad: bfloat16 [512, 49152], P('dp', 'pipe')
- weight_grad: bfloat16 [8, 292, 128, 128], P('pipe', 'dp')
The draws below stay inside these ranges and needn't reach their ends.
Inputs may be any that keep to these rules, and one draw needn't show every extreme that they name: `block_rows`: live slots of slab p list each of its 48 rows of blocks exactly 6 times, with distinct columns; dead slots hold valid indices. `block_cols`: within a row of blocks the live columns are distinct. `block_count`: the counts of one slab sum to 288; in every slab some device holds exactly 73.
All inputs are finite; a program needn't handle non-finite values.
Results may differ from the reference program's by a relative error of at most 0.009.
Values may be sent and summed in bfloat16 or wider, within the bound.
A program may use at most 128 MiB of HBM per device.

```python
import jax
import jax.numpy as jnp
from jax import lax

BLOCK = 128
D = 6144
H = 49152
TOK_DEV = 128
ROW_NNZ = 6
DB = 48
RB = 48
SLAB = 288
CAP = 73
TOKENS = 512
N_DP = 4
N_PIPE = 8


def block_lists(key):
    key_cols = jax.random.fold_in(key, 11)
    key_fill = jax.random.fold_in(key, 12)
    key_full = jax.random.fold_in(key, 13)
    col_keys = jax.random.split(key_cols, N_PIPE * RB)
    columns = jax.vmap(lambda single: jax.random.permutation(single, DB)[:ROW_NNZ])(col_keys)
    columns = columns.reshape(N_PIPE, SLAB).astype(jnp.int32)
    rows_list = jnp.broadcast_to((jnp.arange(SLAB) // ROW_NNZ)[None, :], (N_PIPE, SLAB)).astype(jnp.int32)
    full_shard = jax.random.randint(key_full, (N_PIPE,), 0, N_DP)
    others = (N_DP - 1) * CAP
    fill_keys = jax.random.split(key_fill, N_PIPE)
    ranks = jax.vmap(lambda single: jax.random.permutation(single, others))(fill_keys)
    chosen = (ranks < SLAB - CAP).astype(jnp.int32)
    other_counts = jnp.sum(chosen.reshape(N_PIPE, N_DP - 1, CAP), axis=2)
    shards = jnp.arange(N_DP)[None, :]
    source = shards - (shards > full_shard[:, None]).astype(jnp.int32)
    source = jnp.clip(source, 0, N_DP - 2)
    counts = jnp.where(shards == full_shard[:, None], CAP, jnp.take_along_axis(other_counts, source, axis=1)).astype(jnp.int32)
    starts = jnp.cumsum(counts, axis=1) - counts
    position_index = jnp.arange(N_DP * CAP)
    owners = position_index // CAP
    within = position_index % CAP
    block_ids = (starts[:, owners] + within[None, :]) % SLAB
    slot_rows = jnp.take_along_axis(rows_list, block_ids, axis=1)
    slot_cols = jnp.take_along_axis(columns, block_ids, axis=1)
    return (slot_rows.astype(jnp.int32), slot_cols.astype(jnp.int32), counts)


def draw_block_rows(key, part):
    return block_lists(key)[0]


def draw_block_cols(key, part):
    return block_lists(key)[1]


def draw_block_count(key, part):
    return block_lists(key)[2]


def levels(rng, dims, cuts, least, high):
    level, own = 1.0, jax.random.fold_in(rng, 6)
    for axis_at, parts in cuts:
        steps = jnp.exp(jax.random.uniform(jax.random.fold_in(own, axis_at), (parts,), jnp.float32, least / len(cuts), high / len(cuts)))
        level = level * jnp.repeat(steps, dims[axis_at] // parts).reshape([-1 if axis == axis_at else 1 for axis in range(len(dims))])
    return level


def bell_draw(key, extent, scale, limit, cuts=(), dtype=jnp.bfloat16):
    drawn = jax.random.normal(key, extent, jnp.float32) * scale
    if len(cuts) > 0:
        drawn = levels(key, extent, cuts, -0.22, 0.18) * drawn
    return jnp.clip(drawn, min=-limit, max=limit).astype(dtype)


def setup_inputs(seed: int = 0) -> dict:
    key_list = jax.random.split(jax.random.key(seed), 7)
    return {
        "pre": bell_draw(key_list[0], (TOKENS, H), 1.0, 6.0, ((0, 4), (1, 8))),
        "grad_out": bell_draw(key_list[1], (TOKENS, D), 1.0, 6.0, ((0, 4), (1, 8))),
        "weight_slots": bell_draw(key_list[2], (N_PIPE, N_DP * CAP, BLOCK, BLOCK), (ROW_NNZ * BLOCK) ** -0.5, 0.21875, ((0, 8), (1, 4))),
        "block_rows": draw_block_rows(jax.random.fold_in(key_list[6], 71), 0),
        "block_cols": draw_block_cols(jax.random.fold_in(key_list[6], 71), 0),
        "block_count": draw_block_count(jax.random.fold_in(key_list[6], 71), 0),
    }


inv_root_two = 0.7071067811865476
inverse_square_root_tau = 0.3989422804014327


def gelu_parts(pre_wide):
    normal_cdf = 0.5 * (1.0 + jax.scipy.special.erf(pre_wide * inv_root_two))
    density = jnp.exp(-0.5 * pre_wide * pre_wide) * inverse_square_root_tau
    return pre_wide * normal_cdf, normal_cdf + pre_wide * density


def reference(pre, grad_out, weight_slots, block_rows, block_cols, block_count):
    pre_wide = pre.astype(jnp.float32)
    activation, slopes = gelu_parts(pre_wide)
    activation = activation.astype(jnp.bfloat16)
    slot_total = N_DP * CAP
    grad_blocks = grad_out.reshape(TOKENS, DB, BLOCK)
    position_index = jnp.arange(slot_total)
    live_all = (position_index % CAP)[None, :] < jnp.repeat(block_count, CAP, axis=1)
    row_range = jnp.arange(RB)

    def per_section(section):
        row_ids = block_rows[section]
        col_ids = block_cols[section]
        live_mask = live_all[section].astype(jnp.float32)
        weight_matrix = weight_slots[section].astype(jnp.float32) * live_mask[:, None, None]
        gradient_fragments = grad_blocks[:, col_ids, :].astype(jnp.float32)
        value_portion = jnp.einsum('nbj,baj->nba', gradient_fragments, weight_matrix)
        row_hot = (row_ids[:, None] == row_range[None, :]).astype(jnp.float32)
        hidden_grad = jnp.einsum('tmh,mr->trh', value_portion, row_hot).reshape(TOKENS, RB * BLOCK)
        first = (section * RB * BLOCK).astype(jnp.int32)
        slab_slopes = lax.dynamic_slice_in_dim(slopes, first, RB * BLOCK, 1)
        slab_grad = (hidden_grad * slab_slopes).astype(jnp.bfloat16)
        slab_act = lax.dynamic_slice_in_dim(activation, first, RB * BLOCK, 1).reshape(TOKENS, RB, BLOCK)
        act_pieces = slab_act[:, row_ids, :].astype(jnp.float32)
        terms = jnp.einsum('qtmh,qtmd->qmhd', act_pieces.reshape(N_DP, TOK_DEV, slot_total, BLOCK), gradient_fragments.reshape(N_DP, TOK_DEV, slot_total, BLOCK))
        rounded = lax.optimization_barrier(terms.astype(jnp.bfloat16)).astype(jnp.float32)
        summed = jnp.sum(rounded, axis=0) * live_mask[:, None, None]
        return slab_grad, summed.astype(jnp.bfloat16)

    slab_grads, weight_grad = lax.map(per_section, jnp.arange(N_PIPE).astype(jnp.int32))
    pre_grad = jnp.transpose(slab_grads, (1, 0, 2)).reshape(TOKENS, H)
    return pre_grad, weight_grad
```

```python
import functools

import jax
import jax.numpy as jnp
from jax import lax
from jax.experimental import pallas as pl
from jax.experimental.pallas import tpu as pltpu
from jax.sharding import PartitionSpec as P

BLOCK = 128
UNROLL = 8
MESH = pl.DeviceIdType.MESH

inv_root_two = 0.7071067811865476
inverse_square_root_tau = 0.3989422804014327


def gelu_parts(pre_wide):
    normal_cdf = 0.5 * (1.0 + jax.scipy.special.erf(pre_wide * inv_root_two))
    density = jnp.exp(-0.5 * pre_wide * pre_wide) * inverse_square_root_tau
    return (pre_wide * normal_cdf, normal_cdf + pre_wide * density)


def plain_plan(pre, grad_out, weight_slots, block_rows, block_cols, block_count):
    tok_rows = pre.shape[0]
    slab_rows = pre.shape[1] // BLOCK
    slot_cap = weight_slots.shape[1]
    whole_grad = lax.all_gather(grad_out, "pipe", axis=1, tiled=True)
    grad_blocks = whole_grad.reshape(tok_rows, -1, BLOCK)
    activation, slopes = gelu_parts(pre.astype(jnp.float32))
    activation = activation.astype(jnp.bfloat16)
    act_blocks = activation.reshape(tok_rows, slab_rows, BLOCK)
    row_range = jnp.arange(slab_rows)
    row_ids = lax.all_gather(block_rows, "dp", axis=1, tiled=True)[0]
    col_ids = lax.all_gather(block_cols, "dp", axis=1, tiled=True)[0]
    counts = lax.all_gather(block_count, "dp", axis=1, tiled=True)
    live = jnp.arange(row_ids.shape[0]) % slot_cap < jnp.repeat(counts[0], slot_cap)
    fragments = grad_blocks[:, col_ids, :]
    masked = (
        lax.all_gather(weight_slots, "dp", axis=1, tiled=True)[0]
        * live.astype(jnp.bfloat16)[:, None, None]
    )
    value_portion = jnp.einsum(
        "tkd,khd->tkh", fragments, masked, preferred_element_type=jnp.float32
    )
    row_hot = (row_ids[:, None] == row_range[None, :]).astype(jnp.float32)
    hidden_grad = jnp.einsum("tkh,kr->trh", value_portion, row_hot)
    grad_term = jnp.einsum(
        "tkh,tkd->khd", act_blocks[:, row_ids, :], fragments, preferred_element_type=jnp.float32
    )
    own_grad = lax.psum_scatter(
        (grad_term * live.astype(jnp.float32)[:, None, None]).astype(jnp.bfloat16),
        "dp",
        scatter_dimension=0,
        tiled=True,
    )
    pre_grad = (hidden_grad.reshape(tok_rows, -1) * slopes).astype(jnp.bfloat16)
    return (pre_grad, own_grad[None])


def gather_kernel(depth, cols, grad, pre, weights, meta, g, pre_x, w_core, meta_core,
                  local_sem, chunk_recv, z_send, y_send, x_send, flat_send, flat_recv):
    dp, pipe = lax.axis_index("dp"), lax.axis_index("pipe")
    x, core = dp // 2, dp % 2
    z, y = pipe // 2, pipe % 2
    x_to = ((1 - x) * 2 + core, pipe)
    core_to = (x * 2 + 1 - core, pipe)
    y_to = (dp, z * 2 + 1 - y)
    up_to, down_to = (dp, pipe + 2), (dp, pipe - 2)
    has_up, has_down = z < depth - 1, z > 0

    def greet(who):
        pl.semaphore_signal(barrier, inc=1, device_id=who, device_id_type=MESH)

    def chunk(zz, yy, xx):
        return g.at[pl.ds((zz * 2 + yy) * cols, cols), xx]

    def send(src, dst, send_sem, recv_sem, who):
        return pltpu.make_async_remote_copy(
            src_ref=src, dst_ref=dst, send_sem=send_sem, recv_sem=recv_sem,
            device_id=who, device_id_type=MESH)

    barrier = pltpu.get_barrier_semaphore()
    locals_ = [
        pltpu.make_async_copy(
            grad.at[:, pl.ds(c * BLOCK, BLOCK)], g.at[pipe * cols + c, x], local_sem.at[c])
        for c in range(cols)
    ]
    for copy in locals_:
        copy.start()
    for who in (x_to, core_to, y_to):
        greet(who)

    @pl.when(has_up)
    def _():
        greet(up_to)

    @pl.when(has_down)
    def _():
        greet(down_to)

    pl.semaphore_wait(barrier, 3 + has_up.astype(jnp.int32) + has_down.astype(jnp.int32))
    for copy in locals_:
        copy.wait()
    mine = chunk(z, y, x)
    shard_x = send(mine, mine, x_send.at[0], chunk_recv.at[pipe, x], x_to)
    shard_x.start()
    flat = [
        send(meta, meta_core, flat_send.at[0], flat_recv.at[0], core_to),
        send(weights, w_core, flat_send.at[1], flat_recv.at[1], core_to),
        send(pre, pre_x, flat_send.at[2], flat_recv.at[2], x_to),
    ]
    for copy in flat:
        copy.start()

    def spread(zz, xx, xi, act):
        spot, sem = chunk(zz, y, xx), chunk_recv.at[zz * 2 + y, xx]
        act(send(spot, spot, y_send.at[zz, xx], sem, y_to))

        @pl.when(jnp.logical_and(zz <= z, has_up))
        def _():
            act(send(spot, spot, z_send.at[0, zz, xx], sem, up_to))

        @pl.when(jnp.logical_and(zz >= z, has_down))
        def _():
            act(send(spot, spot, z_send.at[1, zz, xx], sem, down_to))

    def arrived(zz, yy, xx):
        spot, sem = chunk(zz, yy, xx), chunk_recv.at[zz * 2 + yy, xx]
        send(spot, spot, y_send.at[zz, xx], sem, y_to).wait_recv()

    spread(z, x, 0, lambda copy: copy.start())
    arrived(z, y, 1 - x)
    spread(z, 1 - x, 1, lambda copy: copy.start())
    for far in range(1, depth):
        for xi, xx in enumerate((x, 1 - x)):
            for zz, there in ((z - far, z >= far), (z + far, z + far < depth)):
                @pl.when(there)
                def _(zz=zz, xx=xx, xi=xi):
                    arrived(zz, y, xx)
                    spread(zz, xx, xi, lambda copy: copy.start())

    for zz in range(depth):
        for xx in (x, 1 - x):
            arrived(zz, 1 - y, xx)
    for zz in range(depth):
        for xi, xx in enumerate((x, 1 - x)):
            spread(zz, xx, xi, lambda copy: copy.wait_send())
    shard_x.wait_send()
    for copy in flat:
        copy.wait()


def gather(depth, grad, pre, weights, meta):
    cols = grad.shape[1] // BLOCK
    blocks = cols * depth * 2
    any_spec = pl.BlockSpec(memory_space=pl.ANY)
    dma = pltpu.SemaphoreType.DMA
    return pl.pallas_call(
        functools.partial(gather_kernel, depth, cols),
        out_shape=(
            jax.ShapeDtypeStruct((blocks, 2, grad.shape[0], BLOCK), grad.dtype),
            jax.ShapeDtypeStruct(pre.shape, pre.dtype),
            jax.ShapeDtypeStruct(weights.shape, weights.dtype),
            jax.ShapeDtypeStruct(meta.shape, meta.dtype),
        ),
        in_specs=[any_spec] * 4,
        out_specs=(any_spec,) * 4,
        scratch_shapes=[
            dma((cols,)), dma((depth * 2, 2)), dma((2, depth, 2)), dma((depth, 2)),
            dma((1,)), dma((3,)), dma((3,)),
        ],
        compiler_params=pltpu.CompilerParams(collective_id=0, has_side_effects=True),
    )(grad, pre, weights, meta)


def hidden_kernel(cap, group, meta_a, meta_b, w_a, w_b, g, out, acc):
    rows = acc.shape[0] - 1
    acc[...] = jnp.zeros_like(acc)
    for meta, w in ((meta_a, w_a), (meta_b, w_b)):
        count = meta[2 * cap]

        def step(i, carry, meta=meta, w=w, count=count):
            terms = []
            for u in range(UNROLL):
                slot = i * UNROLL + u
                safe = jnp.minimum(slot, cap - 1)
                row = jnp.where(slot < count, meta[safe], rows)
                terms.append((row, lax.dot_general(
                    g[meta[cap + safe], 0], w[safe], (((1,), (1,)), ((), ())),
                    preferred_element_type=jnp.float32)))
            for row, term in terms:
                acc[row] += term
            return carry

        lax.fori_loop(0, pl.cdiv(cap, UNROLL), step, 0)
    for row in range(rows):
        out[:, row * BLOCK:(row + 1) * BLOCK] = acc[row].astype(out.dtype)


def hidden(group, meta_a, meta_b, w_a, w_b, g, rows, dtype):
    cap, tokens = w_a.shape[0], g.shape[2]
    whole = lambda shape: pl.BlockSpec(shape, lambda i, *s: (0,) * len(shape))
    return pl.pallas_call(
        functools.partial(hidden_kernel, cap),
        out_shape=jax.ShapeDtypeStruct((tokens, rows * BLOCK), dtype),
        grid_spec=pltpu.PrefetchScalarGridSpec(
            num_scalar_prefetch=3,
            grid=(1,),
            in_specs=[
                whole(w_a.shape),
                whole(w_b.shape),
                pl.BlockSpec((g.shape[0], 1, tokens, BLOCK), lambda i, group, *s: (0, group[0], 0, 0)),
            ],
            out_specs=whole((tokens, rows * BLOCK)),
            scratch_shapes=[pltpu.VMEM((rows + 1, tokens, BLOCK), jnp.float32)],
        ),
        compiler_params=pltpu.CompilerParams(vmem_limit_bytes=48 << 20),
        cost_estimate=pl.CostEstimate(
            flops=4 * cap * tokens * BLOCK * BLOCK, bytes_accessed=10 << 20, transcendentals=0),
    )(group, meta_a, meta_b, w_a, w_b, g)


def weight_kernel(cap, group, meta_a, meta_b, pre, pre_x, g, out_a, out_b, slopes, act):
    rows, tokens = act.shape[0], pre.shape[0]
    mine = pl.multiple_of(group[0] * tokens, tokens)
    other = pl.multiple_of((1 - group[0]) * tokens, tokens)

    def gelu(row, carry):
        lanes = pl.ds(pl.multiple_of(row * BLOCK, BLOCK), BLOCK)
        value, slope = gelu_parts(pre[:, lanes].astype(jnp.float32))
        slopes[:, lanes] = slope
        act[row, :, pl.ds(mine, tokens)] = value.astype(jnp.bfloat16).T
        value, _ = gelu_parts(pre_x[:, lanes].astype(jnp.float32))
        act[row, :, pl.ds(other, tokens)] = value.astype(jnp.bfloat16).T
        return carry

    lax.fori_loop(0, rows, gelu, 0)
    for meta, out in ((meta_b, out_b), (meta_a, out_a)):
        count = meta[2 * cap]

        def step(i, carry, meta=meta, out=out, count=count):
            for u in range(UNROLL):
                safe = jnp.minimum(i * UNROLL + u, cap - 1)
                piece = g[meta[cap + safe]].reshape(2 * tokens, BLOCK)
                term = jnp.dot(act[meta[safe]], piece, preferred_element_type=jnp.float32)
                out[safe] = jnp.where(safe < count, term, 0.0).astype(out.dtype)
            return carry

        lax.fori_loop(0, pl.cdiv(cap, UNROLL), step, 0)


def weight_terms(group, meta_a, meta_b, pre, pre_x, g, cap):
    tokens, rows = pre.shape[0], pre.shape[1] // BLOCK
    whole = lambda shape: pl.BlockSpec(shape, lambda i, *s: (0,) * len(shape))
    slots = (cap, BLOCK, BLOCK)
    return pl.pallas_call(
        functools.partial(weight_kernel, cap),
        out_shape=(
            jax.ShapeDtypeStruct(slots, jnp.bfloat16),
            jax.ShapeDtypeStruct(slots, jnp.bfloat16),
            jax.ShapeDtypeStruct(pre.shape, jnp.float32),
        ),
        grid_spec=pltpu.PrefetchScalarGridSpec(
            num_scalar_prefetch=3,
            grid=(1,),
            in_specs=[whole(pre.shape), whole(pre_x.shape), whole(g.shape)],
            out_specs=(whole(slots), whole(slots), whole(pre.shape)),
            scratch_shapes=[pltpu.VMEM((rows, BLOCK, 2 * tokens), jnp.bfloat16)],
        ),
        compiler_params=pltpu.CompilerParams(vmem_limit_bytes=48 << 20),
        cost_estimate=pl.CostEstimate(
            flops=8 * cap * tokens * BLOCK * BLOCK, bytes_accessed=16 << 20, transcendentals=0),
    )(group, meta_a, meta_b, pre, pre_x, g)


def pair_plan(depth, pre, grad_out, weight_slots, block_rows, block_cols, block_count):
    rows, cap = pre.shape[1] // BLOCK, weight_slots.shape[1]
    listed = jnp.concatenate([block_rows[0], block_cols[0], block_count[0]])
    meta = jnp.pad(listed, (0, -listed.shape[0] % 1024)).reshape(-1, BLOCK)
    g, pre_x, w_core, meta_core = gather(depth, grad_out, pre, weight_slots[0], meta)
    meta_a, meta_b = meta.reshape(-1), meta_core.reshape(-1)
    group = (lax.axis_index("dp") // 2).astype(jnp.int32).reshape(1)
    far = hidden(1 - group, meta_a, meta_b, weight_slots[0], w_core, g, rows, jnp.bfloat16)
    from_x = lax.ppermute(far, "dp", [(i, (i + 2) % 4) for i in range(4)])
    term_a, term_b, slopes = weight_terms(group, meta_a, meta_b, pre, pre_x, g, cap)
    from_core = lax.ppermute(term_b, "dp", [(i, i ^ 1) for i in range(4)])
    near = hidden(group, meta_a, meta_b, weight_slots[0], w_core, g, rows, jnp.float32)
    weight_grad = (term_a.astype(jnp.float32) + from_core.astype(jnp.float32)).astype(jnp.bfloat16)
    pre_grad = ((near + from_x.astype(jnp.float32)) * slopes).astype(jnp.bfloat16)
    return (pre_grad, weight_grad[None])


def solution(mesh):
    in_specs = (
        P("dp", "pipe"),
        P("dp", "pipe"),
        P("pipe", "dp", None, None),
        P("pipe", "dp"),
        P("pipe", "dp"),
        P("pipe", "dp"),
    )
    out_specs = (P("dp", "pipe"), P("pipe", "dp", None, None))
    paired = mesh.shape["dp"] == 4 and mesh.shape["pipe"] == 8
    plan = functools.partial(pair_plan, mesh.shape["pipe"] // 2) if paired else plain_plan
    return jax.shard_map(
        plan, mesh=mesh, in_specs=in_specs, out_specs=out_specs, check_vma=False
    )
```
